32 devices in a mesh: area: 8 (over z, x), tile: 4 (over y, core).
Axes of the slice: x: 2, y: 2, z: 4, core: 2. Of those that a mesh axis runs over, the one named last changes fastest.
Arguments:
- start_rates: bfloat16 [8, 256, 4096], P('area', None, 'tile'), may hold values from -0.8984375 to 0.8984375
- stim_drive: bfloat16 [8, 256, 4096], P('area', None, 'tile'), may hold values from -6 to 6
- leak_rates: float32 [8, 4096], P('area', 'tile'), may hold values from 0.2 to 0.9
- block_weights: bfloat16 [8, 32, 20, 128, 128], P('area', 'tile'), may hold values from -0.21875 to 0.21875
- near_index: int32 [8, 32, 12], P('area', 'tile'), may hold values from 0 to 9, as said below
- far_index: int32 [8, 32, 8], P('area', 'tile'), may hold values from 0 to 7, as said below
Outputs:
- final_rates: bfloat16 [8, 256, 4096], P('area', None, 'tile')
The draws below stay inside these ranges and needn't reach their ends.
Inputs may be any that keep to these rules, and one draw needn't show every extreme that they name: `near_index`: an entry names one of the tile's own blocks (1 to 8) or the adjacent edge block of the neighbouring tile (0 the lower, 9 the upper). Slot 0 of every tile's first row block is 0 and slot 1 of every tile's last row block is 9. `far_index`: an entry q names the projecting block (the first block) of the same tile in section q, a section of another area; the areas are the consecutive groups of 3, 2, 2 and 1 eighths of the sections, in that order.
All inputs are finite; a program needn't handle non-finite values.
Results may differ from the reference program's by a relative error of at most 0.005.
Values may be sent and summed in bfloat16 or wider, within the bound.
A program may use at most 64 MiB of HBM per device.

```python
import jax
import jax.numpy as jnp
from jax import lax

BLK = 128
RB = 8
K_REC = 12
K_INT = 8
EXPORT = 1
STEPS = 3
BATCH = 256
NEURONS = 4096
N_AREA = 8
N_TILE = 4


def draw_near_index(key, part):
    row_count = N_TILE * RB
    slot_values = jax.random.randint(key, (N_AREA, row_count, K_REC), 0, RB + 2)
    within = jnp.arange(row_count) % RB
    slot_number = jnp.arange(K_REC)
    first_block = (within == 0)[None, :, None] & (slot_number == 0)[None, None, :]
    last_block = (within == RB - 1)[None, :, None] & (slot_number == 1)[None, None, :]
    slot_values = jnp.where(first_block, 0, slot_values)
    slot_values = jnp.where(last_block, RB + 1, slot_values)
    return slot_values.astype(jnp.int32)


def draw_far_index(key, part):
    unit_size = N_AREA // 8
    device_ids = jnp.arange(N_AREA)
    group_start = jnp.where(device_ids >= 7 * unit_size, 7 * unit_size, jnp.where(device_ids >= 5 * unit_size, 5 * unit_size, jnp.where(device_ids >= 3 * unit_size, 3 * unit_size, 0)))
    group_end = jnp.where(device_ids >= 7 * unit_size, 8 * unit_size, jnp.where(device_ids >= 5 * unit_size, 7 * unit_size, jnp.where(device_ids >= 3 * unit_size, 5 * unit_size, 3 * unit_size)))
    own_count = group_end - group_start
    key_device, key_export = jax.random.split(key)
    shape_all = (N_AREA, N_TILE * RB, K_INT)
    upper_bound = jnp.broadcast_to((N_AREA - own_count)[:, None, None], shape_all)
    drawn_rank = jax.random.randint(key_device, shape_all, 0, upper_bound)
    source_device = jnp.where(drawn_rank < group_start[:, None, None], drawn_rank, drawn_rank + own_count[:, None, None])
    export_pick = jax.random.randint(key_export, shape_all, 0, EXPORT)
    return (source_device * EXPORT + export_pick).astype(jnp.int32)


def level_of(stream_key, shape, pieces, smallest, high):
    def one(position, shards_of):
        heights = jax.random.uniform(jax.random.fold_in(jax.random.fold_in(stream_key, 6), position), (shards_of,), jnp.float32, smallest / len(pieces), high / len(pieces))
        return jnp.repeat(jnp.exp(heights), shape[position] // shards_of).reshape((-1,) + (1,) * (len(shape) - position - 1))

    loudness = one(*pieces[0])
    for cut in pieces[1:]:
        loudness = loudness * one(*cut)
    return loudness


def gaussian(stream_key, shape, spread, most, shards=(), kind=jnp.bfloat16):
    result = spread * jax.random.normal(stream_key, shape, jnp.float32)
    if shards:
        result = result * level_of(stream_key, shape, shards, -0.22, 0.18)
    return jnp.clip(result, -most, most).astype(kind)


def setup_inputs(seed: int = 0) -> dict:
    key_list = jax.random.split(jax.random.key(seed), 7)
    start_rates = jnp.clip(jax.random.uniform(key_list[0], (N_AREA, BATCH, NEURONS), jnp.float32, -0.8984375, 0.8984375) * level_of(key_list[0], (N_AREA, BATCH, NEURONS), ((0, 8), (2, 4)), -0.4, 0.0), -0.8984375, 0.8984375).astype(jnp.bfloat16)
    stim_drive = gaussian(key_list[1], (N_AREA, BATCH, NEURONS), 1.0, 6.0, ((0, 8), (2, 4)))
    leak_rates = jnp.clip(0.2 + 0.7 * jax.random.uniform(key_list[2], (N_AREA, NEURONS), jnp.float32) ** level_of(key_list[2], (N_AREA, NEURONS), ((0, 8), (1, 4)), -0.2, 0.2), 0.2, 0.9)
    block_weights = gaussian(key_list[3], (N_AREA, N_TILE * RB, K_REC + K_INT, BLK, BLK), ((K_REC + K_INT) * BLK // 3) ** -0.5, 0.21875, ((0, 8), (1, 4)))
    near_index = draw_near_index(jax.random.fold_in(key_list[6], 71), 0)
    far_index = draw_far_index(jax.random.fold_in(key_list[6], 71), 0)
    return dict(start_rates=start_rates, stim_drive=stim_drive, leak_rates=leak_rates, block_weights=block_weights, near_index=near_index, far_index=far_index)


def reference(start_rates, stim_drive, leak_rates, block_weights, near_index, far_index):
    block_count = N_TILE * RB
    tile_number = jnp.arange(block_count, dtype=jnp.int32) // RB
    near_column = (tile_number * RB)[None, :, None] + near_index
    far_column = (tile_number * (N_AREA * EXPORT))[None, :, None] + far_index
    rates_now = start_rates
    for step_index in range(STEPS):
        grouped = rates_now.reshape(N_AREA, BATCH, N_TILE, RB, BLK)[:, :, :, :EXPORT, :]
        export_pool = jnp.transpose(grouped, (1, 2, 0, 3, 4)).reshape(BATCH, N_TILE * N_AREA * EXPORT, BLK)

        def one_area(area_number):
            area_rates = rates_now[area_number].reshape(BATCH, block_count, BLK)
            edge_zero = jnp.zeros((BATCH, 1, BLK), jnp.bfloat16)
            padded = jnp.concatenate((edge_zero, area_rates, edge_zero), axis=1)
            near_selected = jnp.take(padded, near_column[area_number], axis=1)
            far_selected = jnp.take(export_pool, far_column[area_number], axis=1)
            selected = jnp.concatenate((near_selected, far_selected), axis=2).astype(jnp.float32)
            current = jnp.einsum("brki,rkio->bro", selected, block_weights[area_number].astype(jnp.float32))
            current = current.reshape(BATCH, -1) + stim_drive[area_number].astype(jnp.float32)
            leak_now = leak_rates[area_number]
            updated = (1.0 - leak_now) * rates_now[area_number].astype(jnp.float32) + leak_now * jnp.tanh(current)
            return updated.astype(jnp.bfloat16)

        rates_now = lax.map(one_area, jnp.arange(N_AREA, dtype=jnp.int32))
    return rates_now
```

```python
import functools

import jax
import jax.numpy as jnp
from jax import lax
from jax.experimental import pallas as pl
from jax.experimental.pallas import tpu as pltpu
from jax.sharding import PartitionSpec as P

STEPS = 3
CHUNKS = 2
MESH = pl.DeviceIdType.MESH


def group_of(section, n_area):
    unit = n_area // 8
    return (
        (section >= 3 * unit).astype(jnp.int32)
        + (section >= 5 * unit).astype(jnp.int32)
        + (section >= 7 * unit).astype(jnp.int32)
    )


def kernel(sizes, near_idx, far_idx, rates_hbm, drive_hbm, leak_ref, w_hbm, out_hbm, *scratch):
    n_area, n_tile, batch, rows, k_near, k_far, blk = sizes
    n_col = n_area // 2
    part = batch // CHUNKS
    nears = scratch[:STEPS]
    final = scratch[STEPS]
    scratch = scratch[STEPS + 1 :]
    fars = [scratch[t * CHUNKS : (t + 1) * CHUNKS] for t in range(STEPS)]
    (
        drive, weights, acc,
        load_sem, drive_sem, w_sem, out_sem,
        far_recv, col_send, own_send, relay_send, edge_send, edge_recv,
    ) = scratch[STEPS * CHUNKS :]

    area = lax.axis_index("area")
    tile = lax.axis_index("tile")
    side = lax.rem(area, 2)
    level = area // 2
    partner = area + 1 - 2 * side

    def needs(section, source):
        return group_of(section, n_area) != group_of(source, n_area)

    def column_needs(section, source):
        mate = section + 1 - 2 * lax.rem(section, 2)
        return jnp.logical_or(needs(section, source), needs(mate, source))

    def offsets(far_first):
        steps = range(n_col - 1, 0, -1) if far_first else range(1, n_col)
        return [s * d for d in steps for s in (1, -1)]

    def inside(offset):
        return jnp.logical_and(level + offset >= 0, level + offset < n_col)

    def member(offset):
        return area + 2 * offset

    def span(c):
        return pl.ds(c * part, part)

    def load(r):
        return pltpu.make_async_copy(
            rates_hbm.at[:, pl.ds(r * blk, blk)], nears[0].at[r + 1], load_sem.at[r]
        )

    def load_drive(r):
        return pltpu.make_async_copy(
            drive_hbm.at[:, pl.ds(r * blk, blk)], drive.at[r], drive_sem.at[r]
        )

    def load_weights(r):
        return pltpu.make_async_copy(w_hbm.at[r], weights.at[r], w_sem.at[r])

    order = [0, rows - 1] + list(range(1, rows - 1))
    for r in order:
        load(r).start()
    for r in range(rows):
        load_weights(r).start()
        load_drive(r).start()

    barrier = pltpu.get_barrier_semaphore()
    for offset in offsets(True):
        @pl.when(inside(offset))
        def _(offset=offset):
            pl.semaphore_signal(
                barrier, inc=1, device_id=(member(offset), tile), device_id_type=MESH
            )
    pl.semaphore_signal(barrier, inc=1, device_id=(partner, tile), device_id_type=MESH)
    has_low = tile > 0
    has_high = tile < n_tile - 1

    @pl.when(has_low)
    def _():
        pl.semaphore_signal(barrier, inc=1, device_id=(area, tile - 1), device_id_type=MESH)

    @pl.when(has_high)
    def _():
        pl.semaphore_signal(barrier, inc=1, device_id=(area, tile + 1), device_id_type=MESH)

    for t in range(STEPS):
        @pl.when(jnp.logical_not(has_low))
        def _(t=t):
            nears[t][0] = jnp.zeros((batch, blk), jnp.bfloat16)

        @pl.when(jnp.logical_not(has_high))
        def _(t=t):
            nears[t][rows + 1] = jnp.zeros((batch, blk), jnp.bfloat16)

    pl.semaphore_wait(
        barrier, n_col + has_low.astype(jnp.int32) + has_high.astype(jnp.int32)
    )

    def column_copy(t, c, offset):
        return pltpu.make_async_remote_copy(
            src_ref=nears[t].at[1, span(c)],
            dst_ref=fars[t][c].at[area],
            send_sem=col_send.at[t, c, offset + n_col - 1],
            recv_sem=far_recv.at[t, c, area],
            device_id=(member(offset), tile),
            device_id_type=MESH,
        )

    def own_copy(t, c):
        return pltpu.make_async_remote_copy(
            src_ref=nears[t].at[1, span(c)],
            dst_ref=fars[t][c].at[area],
            send_sem=own_send.at[t, c],
            recv_sem=far_recv.at[t, c, area],
            device_id=(partner, tile),
            device_id_type=MESH,
        )

    def relay_copy(t, c, offset):
        source = member(offset)
        return pltpu.make_async_remote_copy(
            src_ref=fars[t][c].at[source],
            dst_ref=fars[t][c].at[source],
            send_sem=relay_send.at[t, c, offset + n_col - 1],
            recv_sem=far_recv.at[t, c, source],
            device_id=(partner, tile),
            device_id_type=MESH,
        )

    def arrival(t, c, source):
        return pltpu.make_async_remote_copy(
            src_ref=nears[t].at[1, span(c)],
            dst_ref=fars[t][c].at[source],
            send_sem=own_send.at[t, c],
            recv_sem=far_recv.at[t, c, source],
            device_id=(partner, tile),
            device_id_type=MESH,
        )

    def low_copy(t):
        return pltpu.make_async_remote_copy(
            src_ref=nears[t].at[1],
            dst_ref=nears[t].at[rows + 1],
            send_sem=edge_send.at[t, 0],
            recv_sem=edge_recv.at[t, 1],
            device_id=(area, tile - 1),
            device_id_type=MESH,
        )

    def high_copy(t):
        return pltpu.make_async_remote_copy(
            src_ref=nears[t].at[rows],
            dst_ref=nears[t].at[0],
            send_sem=edge_send.at[t, 1],
            recv_sem=edge_recv.at[t, 0],
            device_id=(area, tile + 1),
            device_id_type=MESH,
        )

    def send_export(t, c):
        for offset in offsets(True):
            @pl.when(inside(offset))
            def _(offset=offset):
                @pl.when(column_needs(member(offset), area))
                def _():
                    column_copy(t, c, offset).start()

        @pl.when(needs(partner, area))
        def _():
            own_copy(t, c).start()

    def send_low(t):
        @pl.when(has_low)
        def _():
            low_copy(t).start()

    def send_high(t):
        @pl.when(has_high)
        def _():
            high_copy(t).start()

    def wait_edges(t):
        @pl.when(has_high)
        def _():
            low_copy(t).wait_recv()

        @pl.when(has_low)
        def _():
            high_copy(t).wait_recv()

    def relay(t, c):
        for offset in offsets(False):
            @pl.when(inside(offset))
            def _(offset=offset):
                @pl.when(column_needs(area, member(offset)))
                def _():
                    arrival(t, c, member(offset)).wait_recv()

                @pl.when(needs(partner, member(offset)))
                def _():
                    relay_copy(t, c, offset).start()

    def wait_partner(t, c):
        @pl.when(needs(area, partner))
        def _():
            arrival(t, c, partner).wait_recv()

        for offset in offsets(False):
            @pl.when(inside(offset))
            def _(offset=offset):
                source = partner + 2 * offset

                @pl.when(needs(area, source))
                def _():
                    arrival(t, c, source).wait_recv()

    def chain(pieces, w_of):
        total = None
        for k in range(0, len(pieces), 2):
            pair = jnp.concatenate([p() for p in pieces[k : k + 2]], axis=1)
            term = jnp.dot(pair, w_of(k, pair.shape[1]), preferred_element_type=jnp.float32)
            total = term if total is None else total + term
        return total

    def near_row(t, r):
        pieces = [lambda k=k: nears[t][near_idx[r, k]] for k in range(k_near)]
        total = chain(pieces, lambda k, n: weights[r, pl.ds(k * blk, n), :])
        acc[r] = total + drive[r].astype(jnp.float32)

    def blend(t, r, current, rates):
        leak = leak_ref[r]
        return ((1.0 - leak) * rates.astype(jnp.float32) + leak * jnp.tanh(current)).astype(
            jnp.bfloat16
        )

    def far_row(t, r, chunks):
        if len(chunks) == 1:
            rows_of = span(chunks[0])
        else:
            rows_of = slice(None)
        pieces = [
            lambda k=k: jnp.concatenate([fars[t][c][far_idx[r, k]] for c in chunks], axis=0)
            for k in range(k_far)
        ]
        total = chain(pieces, lambda k, n: weights[r, pl.ds((k_near + k) * blk, n), :])
        value = blend(t, r, acc[r, rows_of, :] + total, nears[t][r + 1, rows_of, :])
        if t + 1 < STEPS:
            nears[t + 1][r + 1, rows_of, :] = value
        else:
            final[r, rows_of, :] = value

    def store(r):
        return pltpu.make_async_copy(
            final.at[r], out_hbm.at[:, pl.ds(r * blk, blk)], out_sem.at[r]
        )

    load(0).wait()
    for c in range(CHUNKS):
        send_export(0, c)
    send_low(0)
    load(rows - 1).wait()
    send_high(0)
    for r in range(1, rows - 1):
        load(r).wait()

    everything = list(range(CHUNKS))
    for t in range(STEPS):
        last = t + 1 == STEPS
        wait_edges(t)

        if t == 0:
            for r in range(rows):
                load_drive(r).wait()
                load_weights(r).wait()

        @pl.loop(0, rows)
        def _(r, t=t):
            near_row(t, r)

        for c in everything:
            relay(t, c)
        if not last:
            for c in everything:
                wait_partner(t, c)
                far_row(t, 0, [c])
                send_export(t + 1, c)
            send_low(t + 1)
            far_row(t, rows - 1, everything)
            send_high(t + 1)

            @pl.loop(1, rows - 1)
            def _(r, t=t):
                far_row(t, r, everything)
        else:
            for c in everything:
                wait_partner(t, c)

            @pl.loop(0, rows)
            def _(r, t=t):
                far_row(t, r, everything)
                store(r).start()

    for r in range(rows):
        store(r).wait()
    for t in range(STEPS):
        for c in everything:
            for offset in offsets(True):
                @pl.when(inside(offset))
                def _(t=t, c=c, offset=offset):
                    @pl.when(column_needs(member(offset), area))
                    def _():
                        column_copy(t, c, offset).wait_send()

                    @pl.when(needs(partner, member(offset)))
                    def _():
                        relay_copy(t, c, offset).wait_send()

            @pl.when(needs(partner, area))
            def _(t=t, c=c):
                own_copy(t, c).wait_send()

        @pl.when(has_low)
        def _(t=t):
            low_copy(t).wait_send()

        @pl.when(has_high)
        def _(t=t):
            high_copy(t).wait_send()


def body(n_area, n_tile, start_rates, stim_drive, leak_rates, block_weights, near_index, far_index):
    _, batch, width = start_rates.shape
    _, rows, slots, blk, _ = block_weights.shape
    k_near, k_far = near_index.shape[-1], far_index.shape[-1]
    sizes = (n_area, n_tile, batch, rows, k_near, k_far, blk)
    n_col = n_area // 2
    part = batch // CHUNKS
    any_spec = pl.BlockSpec(memory_space=pl.ANY)
    smem_spec = pl.BlockSpec(memory_space=pltpu.SMEM)
    vmem_spec = pl.BlockSpec(memory_space=pltpu.VMEM)
    dma = pltpu.SemaphoreType.DMA
    scratch = (
        [pltpu.VMEM((rows + 2, batch, blk), jnp.bfloat16) for _ in range(STEPS)]
        + [pltpu.VMEM((rows, batch, blk), jnp.bfloat16)]
        + [pltpu.VMEM((n_area, part, blk), jnp.bfloat16) for _ in range(STEPS * CHUNKS)]
        + [
            pltpu.VMEM((rows, batch, blk), jnp.bfloat16),
            pltpu.VMEM((rows, slots * blk, blk), jnp.bfloat16),
            pltpu.VMEM((rows, batch, blk), jnp.float32),
            dma((rows,)),
            dma((rows,)),
            dma((rows,)),
            dma((rows,)),
            dma((STEPS, CHUNKS, n_area)),
            dma((STEPS, CHUNKS, 2 * n_col - 1)),
            dma((STEPS, CHUNKS)),
            dma((STEPS, CHUNKS, 2 * n_col - 1)),
            dma((STEPS, 2)),
            dma((STEPS, 2)),
        ]
    )
    out = pl.pallas_call(
        functools.partial(kernel, sizes),
        out_shape=jax.ShapeDtypeStruct((batch, width), jnp.bfloat16),
        in_specs=[smem_spec, smem_spec, any_spec, any_spec, vmem_spec, any_spec],
        out_specs=any_spec,
        scratch_shapes=scratch,
        compiler_params=pltpu.CompilerParams(
            collective_id=0, has_side_effects=True, vmem_limit_bytes=56 * 1024 * 1024
        ),
        name="rate_steps",
    )(
        near_index[0],
        far_index[0],
        start_rates[0],
        stim_drive[0],
        leak_rates[0].reshape(rows, 1, blk),
        block_weights[0].reshape(rows, slots * blk, blk),
    )
    return out[None]


def solution(mesh):
    in_specs = (
        P("area", None, "tile"),
        P("area", None, "tile"),
        P("area", "tile"),
        P("area", "tile", None, None, None),
        P("area", "tile", None),
        P("area", "tile", None),
    )
    out_specs = P("area", None, "tile")
    local = functools.partial(body, mesh.shape["area"], mesh.shape["tile"])
    return jax.shard_map(local, mesh=mesh, in_specs=in_specs, out_specs=out_specs, check_vma=False)
```

```python
import functools

import jax
import jax.numpy as jnp
from jax import lax
from jax.experimental import pallas as pl
from jax.experimental.pallas import tpu as pltpu
from jax.sharding import PartitionSpec as P

STEPS = 3
CHUNKS = 2
LEAD = 1
UNROLL = 2
MESH = pl.DeviceIdType.MESH


def group_of(section, n_area):
    unit = n_area // 8
    return (
        (section >= 3 * unit).astype(jnp.int32)
        + (section >= 5 * unit).astype(jnp.int32)
        + (section >= 7 * unit).astype(jnp.int32)
    )


def kernel(sizes, near_idx, far_idx, rates_hbm, drive_hbm, leak_ref, w_hbm, out_ref, *scratch):
    n_area, n_tile, batch, rows, k_near, k_far, blk = sizes
    n_col = n_area // 2
    part = batch // CHUNKS
    nears = scratch[:STEPS]
    scratch = scratch[STEPS:]
    fars = [scratch[t * CHUNKS : (t + 1) * CHUNKS] for t in range(STEPS)]
    (
        drive, weights, acc,
        load_sem, drive_sem, w_sem,
        far_recv, col_send, own_send, relay_send, edge_send, edge_recv,
    ) = scratch[STEPS * CHUNKS :]

    area = lax.axis_index("area")
    tile = lax.axis_index("tile")
    side = lax.rem(area, 2)
    level = area // 2
    partner = area + 1 - 2 * side

    def needs(section, source):
        return group_of(section, n_area) != group_of(source, n_area)

    def column_needs(section, source):
        mate = section + 1 - 2 * lax.rem(section, 2)
        return jnp.logical_or(needs(section, source), needs(mate, source))

    def offsets(far_first):
        steps = range(n_col - 1, 0, -1) if far_first else range(1, n_col)
        return [s * d for d in steps for s in (1, -1)]

    def inside(offset):
        return jnp.logical_and(level + offset >= 0, level + offset < n_col)

    def member(offset):
        return area + 2 * offset

    def span(c):
        return pl.ds(c * part, part)

    def load(r):
        return pltpu.make_async_copy(
            rates_hbm.at[:, pl.ds(r * blk, blk)], nears[0].at[r + 1], load_sem.at[r]
        )

    def load_drive(r):
        return pltpu.make_async_copy(
            drive_hbm.at[:, pl.ds(r * blk, blk)], drive.at[r], drive_sem.at[r]
        )

    def load_weights(r):
        return pltpu.make_async_copy(w_hbm.at[r], weights.at[r], w_sem.at[r])

    order = [0, rows - 1] + list(range(1, rows - 1))
    for r in order:
        load(r).start()
    for r in range(rows):
        load_weights(r).start()
        load_drive(r).start()

    barrier = pltpu.get_barrier_semaphore()
    for offset in offsets(True):
        @pl.when(inside(offset))
        def _(offset=offset):
            pl.semaphore_signal(
                barrier, inc=1, device_id=(member(offset), tile), device_id_type=MESH
            )
    pl.semaphore_signal(barrier, inc=1, device_id=(partner, tile), device_id_type=MESH)
    has_low = tile > 0
    has_high = tile < n_tile - 1

    @pl.when(has_low)
    def _():
        pl.semaphore_signal(barrier, inc=1, device_id=(area, tile - 1), device_id_type=MESH)

    @pl.when(has_high)
    def _():
        pl.semaphore_signal(barrier, inc=1, device_id=(area, tile + 1), device_id_type=MESH)

    for t in range(STEPS):
        @pl.when(jnp.logical_not(has_low))
        def _(t=t):
            nears[t][0] = jnp.zeros((batch, blk), jnp.bfloat16)

        @pl.when(jnp.logical_not(has_high))
        def _(t=t):
            nears[t][rows + 1] = jnp.zeros((batch, blk), jnp.bfloat16)

    pl.semaphore_wait(
        barrier, n_col + has_low.astype(jnp.int32) + has_high.astype(jnp.int32)
    )

    def column_copy(t, c, offset):
        return pltpu.make_async_remote_copy(
            src_ref=nears[t].at[1, span(c)],
            dst_ref=fars[t][c].at[area],
            send_sem=col_send.at[t, c, offset + n_col - 1],
            recv_sem=far_recv.at[t, c, area],
            device_id=(member(offset), tile),
            device_id_type=MESH,
        )

    def own_copy(t, c):
        return pltpu.make_async_remote_copy(
            src_ref=nears[t].at[1, span(c)],
            dst_ref=fars[t][c].at[area],
            send_sem=own_send.at[t, c],
            recv_sem=far_recv.at[t, c, area],
            device_id=(partner, tile),
            device_id_type=MESH,
        )

    def relay_copy(t, c, offset):
        source = member(offset)
        return pltpu.make_async_remote_copy(
            src_ref=fars[t][c].at[source],
            dst_ref=fars[t][c].at[source],
            send_sem=relay_send.at[t, c, offset + n_col - 1],
            recv_sem=far_recv.at[t, c, source],
            device_id=(partner, tile),
            device_id_type=MESH,
        )

    def arrival(t, c, source):
        return pltpu.make_async_remote_copy(
            src_ref=nears[t].at[1, span(c)],
            dst_ref=fars[t][c].at[source],
            send_sem=own_send.at[t, c],
            recv_sem=far_recv.at[t, c, source],
            device_id=(partner, tile),
            device_id_type=MESH,
        )

    def low_copy(t):
        return pltpu.make_async_remote_copy(
            src_ref=nears[t].at[1],
            dst_ref=nears[t].at[rows + 1],
            send_sem=edge_send.at[t, 0],
            recv_sem=edge_recv.at[t, 1],
            device_id=(area, tile - 1),
            device_id_type=MESH,
        )

    def high_copy(t):
        return pltpu.make_async_remote_copy(
            src_ref=nears[t].at[rows],
            dst_ref=nears[t].at[0],
            send_sem=edge_send.at[t, 1],
            recv_sem=edge_recv.at[t, 0],
            device_id=(area, tile + 1),
            device_id_type=MESH,
        )

    def send_export(t, c):
        for offset in offsets(True):
            @pl.when(inside(offset))
            def _(offset=offset):
                @pl.when(column_needs(member(offset), area))
                def _():
                    column_copy(t, c, offset).start()

        @pl.when(needs(partner, area))
        def _():
            own_copy(t, c).start()

    def send_low(t):
        @pl.when(has_low)
        def _():
            low_copy(t).start()

    def send_high(t):
        @pl.when(has_high)
        def _():
            high_copy(t).start()

    def wait_edges(t):
        @pl.when(has_high)
        def _():
            low_copy(t).wait_recv()

        @pl.when(has_low)
        def _():
            high_copy(t).wait_recv()

    def relay(t, c):
        for offset in offsets(False):
            @pl.when(inside(offset))
            def _(offset=offset):
                @pl.when(column_needs(area, member(offset)))
                def _():
                    arrival(t, c, member(offset)).wait_recv()

                @pl.when(needs(partner, member(offset)))
                def _():
                    relay_copy(t, c, offset).start()

    def wait_partner(t, c):
        @pl.when(needs(area, partner))
        def _():
            arrival(t, c, partner).wait_recv()

        for offset in offsets(False):
            @pl.when(inside(offset))
            def _(offset=offset):
                source = partner + 2 * offset

                @pl.when(needs(area, source))
                def _():
                    arrival(t, c, source).wait_recv()

    def chain(pieces, w_of):
        total = None
        for k in range(0, len(pieces), 2):
            pair = jnp.concatenate([p() for p in pieces[k : k + 2]], axis=1)
            term = jnp.dot(pair, w_of(k, pair.shape[1]), preferred_element_type=jnp.float32)
            total = term if total is None else total + term
        return total

    def near_row(t, r):
        pieces = [lambda k=k: nears[t][near_idx[r, k]] for k in range(k_near)]
        total = chain(pieces, lambda k, n: weights[r, pl.ds(k * blk, n), :])
        acc[r] = total + drive[r].astype(jnp.float32)

    def blend(t, r, current, rates):
        leak = leak_ref[r]
        return ((1.0 - leak) * rates.astype(jnp.float32) + leak * jnp.tanh(current)).astype(
            jnp.bfloat16
        )

    def far_row(t, r, chunks):
        if len(chunks) == 1:
            rows_of = span(chunks[0])
        else:
            rows_of = slice(None)
        pieces = [
            lambda k=k: jnp.concatenate([fars[t][c][far_idx[r, k]] for c in chunks], axis=0)
            for k in range(k_far)
        ]
        total = chain(pieces, lambda k, n: weights[r, pl.ds((k_near + k) * blk, n), :])
        value = blend(t, r, acc[r, rows_of, :] + total, nears[t][r + 1, rows_of, :])
        if t + 1 < STEPS:
            nears[t + 1][r + 1, rows_of, :] = value
        else:
            out_ref[rows_of, pl.ds(pl.multiple_of(r * blk, blk), blk)] = value

    load(0).wait()
    for c in range(CHUNKS):
        send_export(0, c)
    send_low(0)
    load(rows - 1).wait()
    send_high(0)
    for r in range(1, rows - 1):
        load(r).wait()

    everything = list(range(CHUNKS))

    def near_rows(t, first, count):
        @pl.loop(first, first + count, unroll=UNROLL)
        def _(r):
            near_row(t, r)

    def near_part(t):
        wait_edges(t)
        share = rows // 2
        relay(t, 0)
        near_rows(t, 0, share)
        for c in range(1, 1 + LEAD):
            relay(t, c)
        near_rows(t, share, rows - share)

    for r in range(rows):
        load_weights(r).wait()
        load_drive(r).wait()
    near_part(0)
    for t in range(STEPS):
        last = t + 1 == STEPS
        for c in everything:
            wait_partner(t, c)
            if not last:
                far_row(t, 0, [c])
                send_export(t + 1, c)
            if c + 1 + LEAD < CHUNKS:
                relay(t, c + 1 + LEAD)
        if not last:
            send_low(t + 1)
            far_row(t, rows - 1, everything)
            send_high(t + 1)

            @pl.loop(1, rows - 1, unroll=UNROLL)
            def _(r, t=t):
                far_row(t, r, everything)

            near_part(t + 1)
        else:
            @pl.loop(0, rows, unroll=UNROLL)
            def _(r, t=t):
                far_row(t, r, everything)

    for t in range(STEPS):
        for c in everything:
            for offset in offsets(True):
                @pl.when(inside(offset))
                def _(t=t, c=c, offset=offset):
                    @pl.when(column_needs(member(offset), area))
                    def _():
                        column_copy(t, c, offset).wait_send()

                @pl.when(inside(offset))
                def _(t=t, c=c, offset=offset):
                    @pl.when(needs(partner, member(offset)))
                    def _():
                        relay_copy(t, c, offset).wait_send()

            @pl.when(needs(partner, area))
            def _(t=t, c=c):
                own_copy(t, c).wait_send()

        @pl.when(has_low)
        def _(t=t):
            low_copy(t).wait_send()

        @pl.when(has_high)
        def _(t=t):
            high_copy(t).wait_send()


def body(n_area, n_tile, start_rates, stim_drive, leak_rates, block_weights, near_index, far_index):
    _, batch, width = start_rates.shape
    _, rows, slots, blk, _ = block_weights.shape
    k_near, k_far = near_index.shape[-1], far_index.shape[-1]
    sizes = (n_area, n_tile, batch, rows, k_near, k_far, blk)
    n_col = n_area // 2
    part = batch // CHUNKS
    any_spec = pl.BlockSpec(memory_space=pl.ANY)
    smem_spec = pl.BlockSpec(memory_space=pltpu.SMEM)
    vmem_spec = pl.BlockSpec(memory_space=pltpu.VMEM)
    dma = pltpu.SemaphoreType.DMA
    scratch = (
        [pltpu.VMEM((rows + 2, batch, blk), jnp.bfloat16) for _ in range(STEPS)]
        + [pltpu.VMEM((n_area, part, blk), jnp.bfloat16) for _ in range(STEPS * CHUNKS)]
        + [
            pltpu.VMEM((rows, batch, blk), jnp.bfloat16),
            pltpu.VMEM((rows, slots * blk, blk), jnp.bfloat16),
            pltpu.VMEM((rows, batch, blk), jnp.float32),
            dma((rows,)),
            dma((rows,)),
            dma((rows,)),
            dma((STEPS, CHUNKS, n_area)),
            dma((STEPS, CHUNKS, 2 * n_col - 1)),
            dma((STEPS, CHUNKS)),
            dma((STEPS, CHUNKS, 2 * n_col - 1)),
            dma((STEPS, 2)),
            dma((STEPS, 2)),
        ]
    )
    out = pl.pallas_call(
        functools.partial(kernel, sizes),
        out_shape=pltpu.MemorySpace.VMEM((batch, width), jnp.bfloat16),
        in_specs=[smem_spec, smem_spec, any_spec, any_spec, vmem_spec, any_spec],
        out_specs=vmem_spec,
        scratch_shapes=scratch,
        compiler_params=pltpu.CompilerParams(
            collective_id=0, has_side_effects=True, vmem_limit_bytes=56 * 1024 * 1024
        ),
        name="rate_steps",
    )(
        near_index[0],
        far_index[0],
        start_rates[0],
        stim_drive[0],
        leak_rates[0].reshape(rows, 1, blk),
        block_weights[0].reshape(rows, slots * blk, blk),
    )
    return out[None]


def solution(mesh):
    in_specs = (
        P("area", None, "tile"),
        P("area", None, "tile"),
        P("area", "tile"),
        P("area", "tile", None, None, None),
        P("area", "tile", None),
        P("area", "tile", None),
    )
    out_specs = P("area", None, "tile")
    local = functools.partial(body, mesh.shape["area"], mesh.shape["tile"])
    return jax.shard_map(local, mesh=mesh, in_specs=in_specs, out_specs=out_specs, check_vma=False)
```

```python
import functools

import jax
import jax.numpy as jnp
from jax import lax
from jax.experimental import pallas as pl
from jax.experimental.pallas import tpu as pltpu
from jax.sharding import PartitionSpec as P

STEPS = 3
CHUNKS = 2
LEAD = 1
UNROLL = 4
MESH = pl.DeviceIdType.MESH


def group_of(section, n_area):
    unit = n_area // 8
    return (
        (section >= 3 * unit).astype(jnp.int32)
        + (section >= 5 * unit).astype(jnp.int32)
        + (section >= 7 * unit).astype(jnp.int32)
    )


def kernel(sizes, near_idx, far_idx, rates_hbm, drive_hbm, leak_ref, w_hbm, out_ref, *scratch):
    n_area, n_tile, batch, rows, k_near, k_far, blk = sizes
    n_col = n_area // 2
    part = batch // CHUNKS
    nears = scratch[:STEPS]
    scratch = scratch[STEPS:]
    fars = [scratch[t * CHUNKS : (t + 1) * CHUNKS] for t in range(STEPS)]
    (
        drive, weights, acc,
        load_sem, drive_sem, w_sem,
        far_recv, col_send, own_send, relay_send, edge_send, edge_recv,
    ) = scratch[STEPS * CHUNKS :]

    area = lax.axis_index("area")
    tile = lax.axis_index("tile")
    side = lax.rem(area, 2)
    level = area // 2
    partner = area + 1 - 2 * side

    def needs(section, source):
        return group_of(section, n_area) != group_of(source, n_area)

    def column_needs(section, source):
        mate = section + 1 - 2 * lax.rem(section, 2)
        return jnp.logical_or(needs(section, source), needs(mate, source))

    def offsets(far_first):
        steps = range(n_col - 1, 0, -1) if far_first else range(1, n_col)
        return [s * d for d in steps for s in (1, -1)]

    def inside(offset):
        return jnp.logical_and(level + offset >= 0, level + offset < n_col)

    def member(offset):
        return area + 2 * offset

    def span(c):
        return pl.ds(c * part, part)

    def load(r):
        return pltpu.make_async_copy(
            rates_hbm.at[:, pl.ds(r * blk, blk)], nears[0].at[r + 1], load_sem.at[r]
        )

    def load_drive(r):
        return pltpu.make_async_copy(
            drive_hbm.at[:, pl.ds(r * blk, blk)], drive.at[r], drive_sem.at[r]
        )

    def load_weights(r):
        return pltpu.make_async_copy(w_hbm.at[r], weights.at[r], w_sem.at[r])

    order = [0, rows - 1] + list(range(1, rows - 1))
    for r in order:
        load(r).start()
    for r in range(rows):
        load_weights(r).start()
        load_drive(r).start()

    barrier = pltpu.get_barrier_semaphore()
    for offset in offsets(True):
        @pl.when(inside(offset))
        def _(offset=offset):
            pl.semaphore_signal(
                barrier, inc=1, device_id=(member(offset), tile), device_id_type=MESH
            )
    pl.semaphore_signal(barrier, inc=1, device_id=(partner, tile), device_id_type=MESH)
    has_low = tile > 0
    has_high = tile < n_tile - 1

    @pl.when(has_low)
    def _():
        pl.semaphore_signal(barrier, inc=1, device_id=(area, tile - 1), device_id_type=MESH)

    @pl.when(has_high)
    def _():
        pl.semaphore_signal(barrier, inc=1, device_id=(area, tile + 1), device_id_type=MESH)

    for t in range(STEPS):
        @pl.when(jnp.logical_not(has_low))
        def _(t=t):
            nears[t][0] = jnp.zeros((batch, blk), jnp.bfloat16)

        @pl.when(jnp.logical_not(has_high))
        def _(t=t):
            nears[t][rows + 1] = jnp.zeros((batch, blk), jnp.bfloat16)

    pl.semaphore_wait(
        barrier, n_col + has_low.astype(jnp.int32) + has_high.astype(jnp.int32)
    )

    def column_copy(t, c, offset):
        return pltpu.make_async_remote_copy(
            src_ref=nears[t].at[1, span(c)],
            dst_ref=fars[t][c].at[area],
            send_sem=col_send.at[t, c, offset + n_col - 1],
            recv_sem=far_recv.at[t, c, area],
            device_id=(member(offset), tile),
            device_id_type=MESH,
        )

    def own_copy(t, c):
        return pltpu.make_async_remote_copy(
            src_ref=nears[t].at[1, span(c)],
            dst_ref=fars[t][c].at[area],
            send_sem=own_send.at[t, c],
            recv_sem=far_recv.at[t, c, area],
            device_id=(partner, tile),
            device_id_type=MESH,
        )

    def relay_copy(t, c, offset):
        source = member(offset)
        return pltpu.make_async_remote_copy(
            src_ref=fars[t][c].at[source],
            dst_ref=fars[t][c].at[source],
            send_sem=relay_send.at[t, c, offset + n_col - 1],
            recv_sem=far_recv.at[t, c, source],
            device_id=(partner, tile),
            device_id_type=MESH,
        )

    def arrival(t, c, source):
        return pltpu.make_async_remote_copy(
            src_ref=nears[t].at[1, span(c)],
            dst_ref=fars[t][c].at[source],
            send_sem=own_send.at[t, c],
            recv_sem=far_recv.at[t, c, source],
            device_id=(partner, tile),
            device_id_type=MESH,
        )

    def low_copy(t):
        return pltpu.make_async_remote_copy(
            src_ref=nears[t].at[1],
            dst_ref=nears[t].at[rows + 1],
            send_sem=edge_send.at[t, 0],
            recv_sem=edge_recv.at[t, 1],
            device_id=(area, tile - 1),
            device_id_type=MESH,
        )

    def high_copy(t):
        return pltpu.make_async_remote_copy(
            src_ref=nears[t].at[rows],
            dst_ref=nears[t].at[0],
            send_sem=edge_send.at[t, 1],
            recv_sem=edge_recv.at[t, 0],
            device_id=(area, tile + 1),
            device_id_type=MESH,
        )

    def send_export(t, c):
        for offset in offsets(False):
            @pl.when(inside(offset))
            def _(offset=offset):
                @pl.when(column_needs(member(offset), area))
                def _():
                    column_copy(t, c, offset).start()

        @pl.when(needs(partner, area))
        def _():
            own_copy(t, c).start()

    def send_low(t):
        @pl.when(has_low)
        def _():
            low_copy(t).start()

    def send_high(t):
        @pl.when(has_high)
        def _():
            high_copy(t).start()

    def wait_edges(t):
        @pl.when(has_high)
        def _():
            low_copy(t).wait_recv()

        @pl.when(has_low)
        def _():
            high_copy(t).wait_recv()

    def relay(t, c):
        for offset in offsets(False):
            @pl.when(inside(offset))
            def _(offset=offset):
                @pl.when(column_needs(area, member(offset)))
                def _():
                    arrival(t, c, member(offset)).wait_recv()

                @pl.when(needs(partner, member(offset)))
                def _():
                    relay_copy(t, c, offset).start()

    def wait_partner(t, c):
        @pl.when(needs(area, partner))
        def _():
            arrival(t, c, partner).wait_recv()

        for offset in offsets(False):
            @pl.when(inside(offset))
            def _(offset=offset):
                source = partner + 2 * offset

                @pl.when(needs(area, source))
                def _():
                    arrival(t, c, source).wait_recv()

    def chain(pieces, w_of):
        total = None
        for k in range(0, len(pieces), 2):
            pair = jnp.concatenate([p() for p in pieces[k : k + 2]], axis=1)
            term = jnp.dot(pair, w_of(k, pair.shape[1]), preferred_element_type=jnp.float32)
            total = term if total is None else total + term
        return total

    def near_row(t, r):
        pieces = [lambda k=k: nears[t][near_idx[r, k]] for k in range(k_near)]
        total = chain(pieces, lambda k, n: weights[r, pl.ds(k * blk, n), :])
        acc[r] = total + drive[r].astype(jnp.float32)

    def blend(t, r, current, rates):
        leak = leak_ref[r]
        return ((1.0 - leak) * rates.astype(jnp.float32) + leak * jnp.tanh(current)).astype(
            jnp.bfloat16
        )

    def far_row(t, r, chunks):
        if len(chunks) == 1:
            rows_of = span(chunks[0])
        else:
            rows_of = slice(None)
        pieces = [
            lambda k=k: jnp.concatenate([fars[t][c][far_idx[r, k]] for c in chunks], axis=0)
            for k in range(k_far)
        ]
        total = chain(pieces, lambda k, n: weights[r, pl.ds((k_near + k) * blk, n), :])
        value = blend(t, r, acc[r, rows_of, :] + total, nears[t][r + 1, rows_of, :])
        if t + 1 < STEPS:
            nears[t + 1][r + 1, rows_of, :] = value
        else:
            out_ref[rows_of, pl.ds(pl.multiple_of(r * blk, blk), blk)] = value

    load(0).wait()
    for c in range(CHUNKS):
        send_export(0, c)
    send_low(0)
    load(rows - 1).wait()
    send_high(0)
    for r in range(1, rows - 1):
        load(r).wait()

    everything = list(range(CHUNKS))

    def near_rows(t, first, count):
        @pl.loop(first, first + count, unroll=UNROLL)
        def _(r):
            near_row(t, r)

    def near_part(t):
        wait_edges(t)
        share = rows // 2
        relay(t, 0)
        near_rows(t, 0, share)
        for c in range(1, 1 + LEAD):
            relay(t, c)
        near_rows(t, share, rows - share)

    for r in range(rows):
        load_weights(r).wait()
        load_drive(r).wait()
    near_part(0)
    for t in range(STEPS):
        last = t + 1 == STEPS
        for c in everything:
            wait_partner(t, c)
            if last:
                @pl.loop(0, rows, unroll=UNROLL)
                def _(r, t=t, c=c):
                    far_row(t, r, [c])
            if not last:
                far_row(t, 0, [c])
                send_export(t + 1, c)
            if c + 1 + LEAD < CHUNKS:
                relay(t, c + 1 + LEAD)
        if not last:
            send_low(t + 1)
            far_row(t, rows - 1, everything)
            send_high(t + 1)

            @pl.loop(1, rows - 1, unroll=rows - 2)
            def _(r, t=t):
                far_row(t, r, everything)

            near_part(t + 1)

    for t in range(STEPS):
        for c in everything:
            for offset in offsets(True):
                @pl.when(inside(offset))
                def _(t=t, c=c, offset=offset):
                    @pl.when(column_needs(member(offset), area))
                    def _():
                        column_copy(t, c, offset).wait_send()

                @pl.when(inside(offset))
                def _(t=t, c=c, offset=offset):
                    @pl.when(needs(partner, member(offset)))
                    def _():
                        relay_copy(t, c, offset).wait_send()

            @pl.when(needs(partner, area))
            def _(t=t, c=c):
                own_copy(t, c).wait_send()

        @pl.when(has_low)
        def _(t=t):
            low_copy(t).wait_send()

        @pl.when(has_high)
        def _(t=t):
            high_copy(t).wait_send()


def body(n_area, n_tile, start_rates, stim_drive, leak_rates, block_weights, near_index, far_index):
    _, batch, width = start_rates.shape
    _, rows, slots, blk, _ = block_weights.shape
    k_near, k_far = near_index.shape[-1], far_index.shape[-1]
    sizes = (n_area, n_tile, batch, rows, k_near, k_far, blk)
    n_col = n_area // 2
    part = batch // CHUNKS
    any_spec = pl.BlockSpec(memory_space=pl.ANY)
    smem_spec = pl.BlockSpec(memory_space=pltpu.SMEM)
    vmem_spec = pl.BlockSpec(memory_space=pltpu.VMEM)
    dma = pltpu.SemaphoreType.DMA
    scratch = (
        [pltpu.VMEM((rows + 2, batch, blk), jnp.bfloat16) for _ in range(STEPS)]
        + [pltpu.VMEM((n_area, part, blk), jnp.bfloat16) for _ in range(STEPS * CHUNKS)]
        + [
            pltpu.VMEM((rows, batch, blk), jnp.bfloat16),
            pltpu.VMEM((rows, slots * blk, blk), jnp.bfloat16),
            pltpu.VMEM((rows, batch, blk), jnp.float32),
            dma((rows,)),
            dma((rows,)),
            dma((rows,)),
            dma((STEPS, CHUNKS, n_area)),
            dma((STEPS, CHUNKS, 2 * n_col - 1)),
            dma((STEPS, CHUNKS)),
            dma((STEPS, CHUNKS, 2 * n_col - 1)),
            dma((STEPS, 2)),
            dma((STEPS, 2)),
        ]
    )
    out = pl.pallas_call(
        functools.partial(kernel, sizes),
        out_shape=pltpu.MemorySpace.VMEM((batch, width), jnp.bfloat16),
        in_specs=[smem_spec, smem_spec, any_spec, any_spec, vmem_spec, any_spec],
        out_specs=vmem_spec,
        scratch_shapes=scratch,
        compiler_params=pltpu.CompilerParams(
            collective_id=0, has_side_effects=True, vmem_limit_bytes=56 * 1024 * 1024
        ),
        name="rate_steps",
    )(
        near_index[0],
        far_index[0],
        start_rates[0],
        stim_drive[0],
        leak_rates[0].reshape(rows, 1, blk),
        block_weights[0].reshape(rows, slots * blk, blk),
    )
    return out[None]


def solution(mesh):
    in_specs = (
        P("area", None, "tile"),
        P("area", None, "tile"),
        P("area", "tile"),
        P("area", "tile", None, None, None),
        P("area", "tile", None),
        P("area", "tile", None),
    )
    out_specs = P("area", None, "tile")
    local = functools.partial(body, mesh.shape["area"], mesh.shape["tile"])
    return jax.shard_map(local, mesh=mesh, in_specs=in_specs, out_specs=out_specs, check_vma=False)
```
